32 devices in a mesh: clip: 2 (over y), tm: 4 (over x, core), mp: 4 (over z).
Axes of the slice: x: 2, y: 2, z: 4, core: 2. Of those that a mesh axis runs over, the one named last changes fastest.
Arguments:
- token_ids: int32 [8, 256], P(('clip', 'tm')), parts along dimension 0, may hold values from 0 to 1023
- remask: int32 [8, 256], P(('clip', 'tm')), parts along dimension 0, may hold values from -1 to 255, as said below
- position_embed: bfloat16 [4, 256, 1024], P('tm'), may hold values from -0.625 to 0.625
- mask_embed: bfloat16 [1024], replicated, may hold values from -0.625 to 0.625
- table: bfloat16 [1024, 1024], P('mp')
- gain_in: float32 [1024], replicated, may hold values from 0.5 to 1.5
- gain_out: float32 [1024], replicated, may hold values from 0.5 to 1.5
- w_qkv: bfloat16 [3, 1024, 1024], P(None, None, 'mp')
- w_out: bfloat16 [1024, 1024], P('mp'), may hold values from -0.1875 to 0.1875
Outputs:
- log_probs: bfloat16 [8, 256, 1024], P(('clip', 'tm'), None, 'mp'), parts along dimension 0
- confidence: float32 [8, 256], P(('clip', 'tm')), parts along dimension 0
- clip_stats: float32 [4], P('clip'), parts along dimension 0
The draws below stay inside these ranges and needn't reach their ends.
There are 2 independent parts, one for each index of `clip`. The reference program is written for one: setup_inputs(seed, part) draws one part's arguments, and reference() takes and returns one part's arrays. A program takes and returns all parts, laid end to end along the dimension named above; an argument that names none is the same for every part. Nothing has to cross between parts.
Inputs may be any that keep to these rules, and one draw needn't show every extreme that they name: `remask`: row f lists distinct masked positions of frame f in its first slots and -1 in the unused ones; every frame lists at least one position.
All inputs are finite; a program needn't handle non-finite values.
Results may differ from the reference program's by a relative error of at most 0.019.
The reference program's roundings to bfloat16 on the way (of `normed`, `context` and `final_rows`) count: a program that leaves them out, or rounds other values in their place, can miss the bound.
Values may be sent and summed in bfloat16 or wider, within the bound.
No kernel may reach another device: no remote copies, remote signals or barrier semaphores. Data moves between devices by JAX's collectives and lax.ppermute only.
A program may use at most 64 MiB of HBM per device.

```python
import math
import jax
import jax.numpy as jnp
import numpy as np
from jax import lax

D = 1024
HEADS = 16
VOCAB = 1024
HEAD_DIM = 64
SPAN = 256
FRAMES = 4
TOKENS = 1024
SLOTS = 256


def draw_remask(key, part):
    pick_key = jax.random.fold_in(key, 3)
    spread_key = jax.random.fold_in(key, 5)
    steps_all = max(FRAMES - 1, 1)
    base_counts = [max(1, int(SPAN / 64.0 * 64.0 ** (frame / steps_all) + 0.5)) for frame in range(FRAMES)]
    live_count = jnp.array(base_counts, dtype=jnp.int32)
    live_count = live_count + jax.random.randint(spread_key, (FRAMES,), 0, SPAN // 64 + 1)
    live_count = jnp.minimum(live_count, SLOTS)
    scores = jax.random.randint(pick_key, (FRAMES, SPAN), 0, 65536) * SPAN + jnp.arange(SPAN, dtype=jnp.int32)[None, :]
    places = jnp.argsort(scores, axis=-1, stable=True).astype(jnp.int32)
    slot_ids = jnp.arange(SLOTS, dtype=jnp.int32)
    return jnp.where(slot_ids[None, :] < live_count[:, None], places, -1).astype(jnp.int32)


def draw_table(key, part):
    base = jax.random.normal(key, (VOCAB, D), jnp.float32) * 0.1
    return base.astype(jnp.bfloat16)


def draw_w_qkv(key, part):
    base = jax.random.normal(key, (3, D, D), jnp.float32) * D ** (-0.5)
    return base.astype(jnp.bfloat16)


def touch_ends(drawn, rng, smallest, high):
    shape = drawn.shape
    spot = [jax.random.randint(jax.random.fold_in(rng, axis), (), 0, shape[axis]) for axis in range(len(shape))]
    drawn = drawn.at[tuple(spot)].set(smallest)
    longest = shape.index(max(shape))
    spot[longest] = (spot[longest] + 1) % shape[longest]
    return drawn.at[tuple(spot)].set(high)


def shard_levels(rng, extent, split, low, largest):
    factor_of = 1.0
    for position, blocks in split:
        steps = jax.random.uniform(jax.random.fold_in(jax.random.fold_in(rng, 6), position), (blocks,), jnp.float32, low / len(split), largest / len(split))
        factor_of = factor_of * jnp.repeat(jnp.exp(steps), extent[position] // blocks).reshape((-1,) + (1,) * (len(extent) - 1 - position))
    return factor_of


def cumulative_ranks(amount, slope):
    weights = [(1 << 20) // math.isqrt(standing ** slope) + 1 for standing in range(1, amount + 1)]
    scale = 1 + sum(weights) // (1 << 30)
    return np.cumsum(np.array([max(1, weight // scale) for weight in weights]))


def ranked(key, shape, amount, lean):
    listing = cumulative_ranks(amount, lean)
    pick = jax.random.randint(jax.random.fold_in(key, 1), shape, 0, int(listing[amount - 1]))
    rank = jnp.searchsorted(jnp.asarray(listing, jnp.int32), pick, side="right")
    return jax.random.permutation(jax.random.fold_in(key, 2), amount)[rank].astype(jnp.int32)


def noise(own_key, shape, scale, reach, cuts=(), held_as=jnp.bfloat16):
    factor_of = shard_levels(own_key, shape, cuts, -0.22, 0.18) if cuts else 1.0
    values = jax.random.normal(own_key, shape, jnp.float32) * scale * factor_of
    return jnp.minimum(jnp.maximum(values, -reach), reach).astype(held_as)


def setup_inputs(seed: int = 0, part: int = 0) -> dict:
    arg_keys = jax.random.split(jax.random.key(seed), 10)
    own_keys = jax.random.split(jax.random.fold_in(arg_keys[9], part), 10)
    return {
        "token_ids": touch_ends(ranked(own_keys[0], (FRAMES, SPAN), VOCAB, 2), jax.random.fold_in(own_keys[0], 3), 0, VOCAB - 1).astype(jnp.int32),
        "remask": draw_remask(jax.random.fold_in(jax.random.fold_in(arg_keys[9], part), 71), part),
        "position_embed": noise(arg_keys[2], (FRAMES, SPAN, D), 0.1, 0.625, ((0, 4),)),
        "mask_embed": noise(arg_keys[3], (D,), 0.1, 0.625),
        "table": draw_table(jax.random.fold_in(arg_keys[9], 71), part),
        "gain_in": jnp.clip(1.0 + 0.1 * jax.random.normal(arg_keys[5], (D,), jnp.float32), 0.5, 1.5),
        "gain_out": jnp.clip(1.0 + 0.1 * jax.random.normal(arg_keys[6], (D,), jnp.float32), 0.5, 1.5),
        "w_qkv": draw_w_qkv(jax.random.fold_in(arg_keys[9], 71), part),
        "w_out": noise(arg_keys[8], (D, D), D ** -0.5, 0.1875, ((0, 4),)),
    }


def layer_norm(values, gain):
    center = values - lax.optimization_barrier(jnp.mean(values, axis=-1, keepdims=True))
    spread = lax.optimization_barrier(jnp.mean(center * center, axis=-1, keepdims=True))
    return center * lax.rsqrt(spread + 1e-05) * gain

def attend_head(trio):
    query, keys, values = trio
    blocks = query.reshape(FRAMES, SPAN, HEAD_DIM)

    def one_block(block):
        scores = jnp.dot(block, keys.T, preferred_element_type=jnp.float32) * HEAD_DIM ** (-0.5)
        highest = lax.optimization_barrier(jnp.max(scores, axis=-1, keepdims=True))
        weights = jnp.exp(scores - highest)
        summed = jnp.dot(weights.astype(jnp.bfloat16), values, preferred_element_type=jnp.float32)
        return summed / lax.optimization_barrier(jnp.sum(weights, axis=-1, keepdims=True))
    return lax.map(one_block, blocks).reshape(TOKENS, HEAD_DIM)

def reference(token_ids, remask, position_embed, mask_embed, table, gain_in, gain_out, w_qkv, w_out):
    positions = jnp.arange(SPAN, dtype=jnp.int32)
    masked = jnp.any(remask[:, None, :] == positions[None, :, None], axis=-1)
    looked = jnp.take(table, token_ids, axis=0).astype(jnp.float32)
    hidden_in = jnp.where(masked[:, :, None], mask_embed.astype(jnp.float32)[None, None, :], looked)
    hidden_in = (hidden_in + position_embed.astype(jnp.float32)).reshape(TOKENS, D)
    normed = layer_norm(hidden_in, gain_in).astype(jnp.bfloat16)
    query = jnp.dot(normed, w_qkv[0], preferred_element_type=jnp.float32).astype(jnp.bfloat16)
    keys = jnp.dot(normed, w_qkv[1], preferred_element_type=jnp.float32).astype(jnp.bfloat16)
    values = jnp.dot(normed, w_qkv[2], preferred_element_type=jnp.float32).astype(jnp.bfloat16)
    heads_query = query.reshape(TOKENS, HEADS, HEAD_DIM).transpose(1, 0, 2)
    heads_keys = keys.reshape(TOKENS, HEADS, HEAD_DIM).transpose(1, 0, 2)
    heads_values = values.reshape(TOKENS, HEADS, HEAD_DIM).transpose(1, 0, 2)
    context = lax.map(attend_head, (heads_query, heads_keys, heads_values))
    context = context.transpose(1, 0, 2).reshape(TOKENS, D).astype(jnp.bfloat16)
    mixed_rows = jnp.dot(context, w_out, preferred_element_type=jnp.float32)
    final_rows = layer_norm(hidden_in + mixed_rows, gain_out).astype(jnp.bfloat16)
    logits = jnp.dot(final_rows, table.T, preferred_element_type=jnp.float32)
    highest = lax.optimization_barrier(jnp.max(logits, axis=-1, keepdims=True))
    log_total = highest + jnp.log(lax.optimization_barrier(jnp.sum(jnp.exp(logits - highest), axis=-1, keepdims=True)))
    log_probs = (logits - log_total).astype(jnp.bfloat16).reshape(FRAMES, SPAN, VOCAB)
    confidence = jnp.exp(highest - log_total).reshape(TOKENS)
    weight = masked.reshape(TOKENS).astype(jnp.float32)
    count = jnp.sum(weight)
    clip_stats = jnp.stack([jnp.sum(confidence * weight) / count, jnp.log(count / TOKENS)])
    return (log_probs, confidence.reshape(FRAMES, SPAN), clip_stats)
```

```python
import functools

import jax
import jax.numpy as jnp
from jax import lax
from jax.experimental import pallas as pl
from jax.experimental.pallas import tpu as pltpu
from jax.sharding import PartitionSpec as P

HEAD_DIM = 64
PLANE = ("clip", "tm")
NT = (((1,), (1,)), ((), ()))


def shape(dims, dtype):
    return jax.ShapeDtypeStruct(dims, dtype)


def layer_norm(values, gain):
    center = values - jnp.mean(values, axis=-1, keepdims=True)
    spread = jnp.mean(center * center, axis=-1, keepdims=True)
    return center * lax.rsqrt(spread + 1e-05) * gain


def flip(value, mask, count):
    return lax.ppermute(value, PLANE, [(i, i ^ mask) for i in range(count)])


def turn(value, shift, parts):
    return lax.ppermute(value, "mp", [(i, (i + shift) % parts) for i in range(parts)])


def front_kernel(ids_ref, masked_ref, vocab_ref, own_ref, near_ref, far_ref, place_ref, embed_ref,
                 gain_ref, w_ref, query_ref, pair_ref, mine_ref, held):
    ids = ids_ref[...]
    first = 0
    looked = None
    for part in (own_ref, near_ref, far_ref):
        rows = part.shape[0]
        onehot = jnp.where(ids == vocab_ref[:, first:first + rows], 1.0, 0.0).astype(jnp.bfloat16)
        term = jnp.dot(onehot, part[...], preferred_element_type=jnp.float32)
        looked = term if looked is None else looked + term
        first += rows
    hidden = jnp.where(masked_ref[...] > 0, embed_ref[...].astype(jnp.float32), looked)
    hidden = hidden + place_ref[...].astype(jnp.float32)
    held[...] = hidden
    normed = layer_norm(hidden, gain_ref[...]).astype(jnp.bfloat16)
    width = w_ref.shape[2]
    query = jnp.dot(normed, w_ref[0], preferred_element_type=jnp.float32)
    query_ref[...] = query.astype(jnp.bfloat16)
    for j in range(2):
        rows = jnp.dot(normed, w_ref[j + 1], preferred_element_type=jnp.float32)
        pair_ref[:, j * width:(j + 1) * width] = rows.astype(jnp.bfloat16)
    share = mine_ref.shape[0]
    start = pl.multiple_of(lax.axis_index("mp") * share, share)
    mine_ref[...] = held[pl.ds(start, share), :]


def attend_kernel(query_ref, *refs):
    parts = lax.axis_size("mp")
    blocks, w_ref, outs, total = refs[:-parts - 2], refs[-parts - 2], refs[-parts - 1:-1], refs[-1]
    rows, width = query_ref.shape
    lanes = 2 * HEAD_DIM
    column = lax.broadcasted_iota(jnp.int32, (rows, lanes), 1)
    context = []
    for first in range(0, width, lanes):
        query = query_ref[:, first:first + lanes] * jnp.bfloat16(HEAD_DIM ** -0.5)
        pair = []
        for head in range(2):
            here = (column < HEAD_DIM) if head == 0 else (column >= HEAD_DIM)
            asked = jnp.where(here, query, jnp.zeros_like(query))
            scores = [
                lax.dot_general(asked, ref[:, first:first + lanes], NT, preferred_element_type=jnp.float32)
                for ref in blocks
            ]
            highest = functools.reduce(jnp.maximum, [jnp.max(s, axis=-1, keepdims=True) for s in scores])
            weights = [jnp.exp(s - highest) for s in scores]
            summed = sum(jnp.sum(w, axis=-1, keepdims=True) for w in weights)
            mixed = sum(
                jnp.dot(w.astype(jnp.bfloat16), ref[:, width + first:width + first + lanes],
                        preferred_element_type=jnp.float32)
                for w, ref in zip(weights, blocks)
            )
            pair.append(mixed / summed)
        context.append(jnp.where(column < HEAD_DIM, pair[0], pair[1]).astype(jnp.bfloat16))
    total[...] = jnp.dot(jnp.concatenate(context, axis=1), w_ref[...], preferred_element_type=jnp.float32)
    me = lax.axis_index("mp")
    for shift, out in enumerate(outs):
        share = out.shape[0]
        start = pl.multiple_of(lax.rem(me + shift, parts) * share, share)
        out[...] = total[pl.ds(start, share), :].astype(out.dtype)


def final_kernel(mine_ref, hidden_ref, gain_ref, table_ref, *refs):
    parts = lax.axis_size("mp")
    others, outs, held = refs[:parts - 1], refs[parts - 1:-1], refs[-1]
    mixed = mine_ref[...]
    for other in others:
        mixed = mixed + other[...].astype(jnp.float32)
    rows = layer_norm(hidden_ref[...] + mixed, gain_ref[...]).astype(jnp.bfloat16)
    logits = lax.dot_general(rows, table_ref[...], NT, preferred_element_type=jnp.float32)
    highest = jnp.max(logits, axis=-1, keepdims=True)
    log_total = highest + jnp.log(jnp.sum(jnp.exp(logits - highest), axis=-1, keepdims=True))
    held[...] = (logits - log_total).astype(jnp.bfloat16)
    confidence = jnp.exp(highest - log_total)
    share = logits.shape[0]
    width = outs[0].shape[1]
    me = lax.axis_index("mp")
    row = lax.broadcasted_iota(jnp.int32, (share, width), 0) + me * share
    lane = lax.broadcasted_iota(jnp.int32, (share, width), 1)
    line = jnp.sum(jnp.where(row == lane, confidence, 0.0), axis=0, keepdims=True)
    high = line.astype(jnp.bfloat16)
    rest = line - high.astype(jnp.float32)
    middle = rest.astype(jnp.bfloat16)
    low = (rest - middle.astype(jnp.float32)).astype(jnp.bfloat16)
    extra = outs[0].shape[0] - share
    place = lax.broadcasted_iota(jnp.int32, (extra, width), 0)
    tail = jnp.where(place == 0, high.astype(jnp.float32),
                     jnp.where(place == 1, middle.astype(jnp.float32),
                               jnp.where(place == 2, low.astype(jnp.float32), 0.0))).astype(jnp.bfloat16)
    for shift, out in enumerate(outs):
        start = pl.multiple_of(lax.rem(me + shift, parts) * width, width)
        out[:share, :] = held[:, pl.ds(start, width)]
        out[share:, :] = tail


def close_kernel(masked_ref, *refs):
    parts = lax.axis_size("mp")
    pieces, log_ref, conf_ref, sums_ref = refs[:parts], refs[-3], refs[-2], refs[-1]
    me = lax.axis_index("mp")
    share = log_ref.shape[0] // parts
    line = None
    for shift, piece in enumerate(pieces):
        start = pl.multiple_of(lax.rem(me + parts - shift, parts) * share, share)
        log_ref[pl.ds(start, share), :] = piece[:share, :]
        tail = piece[share:, :].astype(jnp.float32)
        term = jnp.sum(tail, axis=0, keepdims=True)
        line = term if line is None else line + term
    conf_ref[...] = line
    weight = masked_ref[...]
    lanes = sums_ref.shape[1]
    side = lax.broadcasted_iota(jnp.int32, (1, lanes), 1)
    sums_ref[...] = jnp.where(
        side == 0, jnp.sum(line * weight), jnp.where(side == 1, jnp.sum(weight), 0.0)
    )


def body(token_ids, remask, position_embed, mask_embed, table, gain_in, gain_out, w_qkv, w_out):
    bf16, f32 = jnp.bfloat16, jnp.float32
    frames_here, span = token_ids.shape
    rows = frames_here * span
    parts = lax.axis_size("mp")
    clips, tms = lax.axis_size("clip"), lax.axis_size("tm")
    plane = clips * tms
    clip, tm, me = lax.axis_index("clip"), lax.axis_index("tm"), lax.axis_index("mp")
    vocab_here, depth = table.shape
    width = w_qkv.shape[2]
    share = rows // parts

    masks = [m for m in (1, 2) if tms % (2 * m) == 0] + ([tms] if clips % 2 == 0 else [])
    spot = clip * tms + tm
    piece = sum(jnp.where((spot & m) > 0, 1 << b, 0) for b, m in enumerate(masks))
    cuts = 1 << len(masks)
    cut = vocab_here // cuts

    sent = lax.dynamic_slice_in_dim(table, piece * cut, cut, 0)
    got = jnp.concatenate([turn(sent, s, parts) for s in range(1, parts)], axis=0)
    combos = [c for c in range(0, cuts, 2)]
    near = [got]
    for c in combos[1:]:
        mask = sum(m for b, m in enumerate(masks) if c >> b & 1)
        near.append(flip(got, mask, plane))
    near = jnp.concatenate(near, axis=0)
    far = flip(near, masks[0], plane)

    sources = jnp.stack([(me + parts - s) % parts for s in range(1, parts)])
    inner = jnp.arange(cut, dtype=jnp.int32)

    def listing(odd):
        rows_of = [piece ^ (c + odd) for c in combos]
        return jnp.concatenate([
            (sources[:, None] * vocab_here + p * cut + inner[None, :]).reshape(-1) for p in rows_of
        ])

    vocab = jnp.concatenate(
        [me * vocab_here + jnp.arange(vocab_here, dtype=jnp.int32), listing(0), listing(1)]
    ).astype(jnp.int32)[None, :]

    spots = jnp.arange(span, dtype=jnp.int32)
    masked = jnp.any(remask[:, None, :] == spots[None, :, None], axis=-1).reshape(rows)
    weight = masked.astype(f32)
    ids = jnp.where(masked, -1, token_ids.reshape(rows))

    query, pair, mine = pl.pallas_call(
        front_kernel,
        out_shape=[shape((rows, width), bf16), shape((rows, 2 * width), bf16), shape((share, depth), f32)],
        scratch_shapes=[pltpu.VMEM((rows, depth), f32)],
    )(ids[:, None], masked.astype(jnp.int32)[:, None], vocab, table, near, far,
      position_embed.reshape(rows, depth), mask_embed[None, :], gain_in[None, :], w_qkv)

    blocks = [pair]
    mask = tms // 2
    held = pair
    while mask >= 1:
        other = flip(held, mask, plane)
        blocks.append(other)
        held = jnp.concatenate([held, other], axis=0)
        mask //= 2

    whole = jnp.zeros((parts * vocab_here, depth), bf16)
    whole = lax.dynamic_update_slice(whole, table, (me * vocab_here, 0))
    for odd, part in ((0, near), (1, far)):
        chunks = part.reshape(len(combos), parts - 1, cut, depth)
        for i, c in enumerate(combos):
            for s in range(1, parts):
                at = ((me + parts - s) % parts) * vocab_here + (piece ^ (c + odd)) * cut
                whole = lax.dynamic_update_slice(whole, chunks[i, s - 1], (at, 0))

    sums = pl.pallas_call(
        attend_kernel,
        out_shape=[shape((share, depth), f32)] + [shape((share, depth), bf16)] * (parts - 1),
        scratch_shapes=[pltpu.VMEM((rows, depth), f32)],
    )(query, *blocks, w_out)
    others = [turn(sums[s], s, parts) for s in range(1, parts)]

    extra = 16
    notes = pl.pallas_call(
        final_kernel,
        out_shape=[shape((share + extra, vocab_here), bf16)] * parts,
        scratch_shapes=[pltpu.VMEM((share, parts * vocab_here), bf16)],
    )(sums[0], mine, gain_out[None, :], whole, *others)
    notes = [notes[0]] + [turn(notes[s], s, parts) for s in range(1, parts)]
    log_probs, confidence, stats = pl.pallas_call(
        close_kernel,
        out_shape=[shape((rows, vocab_here), bf16), shape((1, rows), f32), shape((1, 128), f32)],
    )(weight[None, :], *notes)
    mask = 1
    while mask < tms:
        stats = stats + flip(stats, mask, plane)
        mask *= 2
    conf_sum, count = stats[0, 0], stats[0, 1]
    clip_stats = jnp.stack([conf_sum / count, jnp.log(count / (rows * tms))])
    return (
        log_probs.reshape(frames_here, span, vocab_here),
        confidence.reshape(frames_here, span),
        clip_stats,
    )


def solution(mesh):
    return jax.shard_map(
        body,
        mesh=mesh,
        in_specs=(
            P(("clip", "tm"), None),
            P(("clip", "tm"), None),
            P("tm", None, None),
            P(),
            P("mp", None),
            P(),
            P(),
            P(None, None, "mp"),
            P("mp", None),
        ),
        out_specs=(P(("clip", "tm"), None, "mp"), P(("clip", "tm"), None), P("clip")),
        check_vma=False,
    )
```
